32 devices in a mesh: groups: 2 (over y), lx: 16 (over z, x, core).
Axes of the slice: x: 2, y: 2, z: 4, core: 2. Of those that a mesh axis runs over, the one named last changes fastest.
Arguments:
- syndrome: int32 [32, 2048], P(('groups', 'lx')), parts along dimension 0, may hold values 0 or 1
- events: int32 [32, 2048], P(('groups', 'lx')), parts along dimension 0, may hold values 0 or 1
- boundary: int32 [32, 2048], P(('groups', 'lx')), parts along dimension 0, may hold values from 0 to 3
- syn_table: float32 [2, 256], replicated, may hold values from -3 to 3
- event_table: float32 [2, 256], replicated, may hold values from -3 to 3
- bound_table: float32 [4, 256], replicated, may hold values from -3 to 3
- pos_table: float32 [64, 256], replicated, may hold values from -3 to 3
- norm_attn: float32 [2, 256], replicated, may hold values from 0.1 to 1.9
- w_query: bfloat16 [2, 256, 256], replicated, may hold values from -18 to 18
- w_key: bfloat16 [2, 256, 256], replicated, may hold values from -0.375 to 0.375
- w_value: bfloat16 [2, 256, 256], replicated, may hold values from -0.375 to 0.375
- w_out: bfloat16 [2, 256, 256], replicated, may hold values from -0.75 to 0.75
- norm_mlp: float32 [2, 256], replicated, may hold values from 0.1 to 1.9
- w_up: bfloat16 [2, 256, 1024], replicated, may hold values from -0.375 to 0.375
- w_down: bfloat16 [2, 1024, 256], replicated, may hold values from -0.25 to 0.25
- norm_final: float32 [256], replicated, may hold values from 0.1 to 1.9
- w_read: bfloat16 [256, 2], replicated, may hold values from -0.375 to 0.375
Outputs:
- logits: float32 [2, 32, 2048], P(None, ('groups', 'lx')), parts along dimension 1
The draws below stay inside these ranges and needn't reach their ends.
There are 2 independent parts, one for each index of `groups`. The reference program is written for one: setup_inputs(seed, part) draws one part's arguments, and reference() takes and returns one part's arrays. A program takes and returns all parts, laid end to end along the dimension named above; an argument that names none is the same for every part. Nothing has to cross between parts.
All inputs are finite; a program needn't handle non-finite values. No bound on the sum of `syndrome` or of `events` on one device may be relied on, other than what follows from the above.
Results may differ from the reference program's by a relative error of at most 0.029.
The reference program's roundings to bfloat16 on the way (of `normed`, `weights`, `attended`, `inner` and `final`) count: a program that leaves them out, or rounds other values in their place, can miss the bound.
Values may be sent and summed in bfloat16 or wider, within the bound.
A program may use at most 192 MiB of HBM per device.

```python
import math
import jax
import jax.numpy as jnp
from jax import lax

D = 256
HEADS = 8
FF = 1024
TILE = 64
LAYERS = 2
NXT = 16
NSITE = 2048


def draw_w_query(key, part):
    first = jax.random.fold_in(jax.random.fold_in(key, 11), 0)
    base = jax.random.truncated_normal(first, -4.0, 4.0, (LAYERS, D, D), jnp.float32) * (3.0 / math.sqrt(D))
    return base.astype(jnp.bfloat16)


def touch_ends(result, rng, low, top_value):
    shape = result.shape
    place = [jax.random.randint(jax.random.fold_in(rng, axis), (), 0, shape[axis]) for axis in range(len(shape))]
    result = result.at[tuple(place)].set(low)
    longest = shape.index(max(shape))
    place[longest] = (place[longest] + 1) % shape[longest]
    return result.at[tuple(place)].set(top_value)


def gaussian(stream_key, extent, scale, bound, kind=jnp.bfloat16):
    result = scale * jax.random.normal(stream_key, extent, jnp.float32)
    return jnp.clip(result, min=-bound, max=bound).astype(kind)


def setup_inputs(seed: int = 0, part: int = 0) -> dict:
    splits = jax.random.split(jax.random.key(seed), 18)
    part_keys = jax.random.split(jax.random.fold_in(splits[17], part), 18)
    return {
        "syndrome": touch_ends((jax.random.randint(part_keys[0], (NXT, NSITE), 0, 2) < 1).astype(jnp.int32), jax.random.fold_in(part_keys[0], 1), 0, 1),
        "events": touch_ends((jax.random.randint(part_keys[1], (NXT, NSITE), 0, 4) < 1).astype(jnp.int32), jax.random.fold_in(part_keys[1], 1), 0, 1),
        "boundary": touch_ends(jax.random.randint(part_keys[2], (NXT, NSITE), 0, 4), jax.random.fold_in(part_keys[2], 1), 0, 3).astype(jnp.int32),
        "syn_table": gaussian(splits[3], (2, D), 0.5, 3.0, jnp.float32),
        "event_table": gaussian(splits[4], (2, D), 0.5, 3.0, jnp.float32),
        "bound_table": gaussian(splits[5], (4, D), 0.5, 3.0, jnp.float32),
        "pos_table": gaussian(splits[6], (TILE, D), 0.5, 3.0, jnp.float32),
        "norm_attn": jnp.clip(1.0 + 0.18 * jax.random.normal(splits[7], (LAYERS, D), jnp.float32), 0.1, 1.9),
        "w_query": draw_w_query(jax.random.fold_in(splits[17], 71), part),
        "w_key": gaussian(splits[9], (LAYERS, D, D), D ** -0.5, 0.375),
        "w_value": gaussian(splits[10], (LAYERS, D, D), D ** -0.5, 0.375),
        "w_out": gaussian(splits[11], (LAYERS, D, D), (D // 4) ** -0.5, 0.75),
        "norm_mlp": jnp.clip(1.0 + 0.18 * jax.random.normal(splits[12], (LAYERS, D), jnp.float32), 0.1, 1.9),
        "w_up": gaussian(splits[13], (LAYERS, D, FF), D ** -0.5, 0.375),
        "w_down": gaussian(splits[14], (LAYERS, FF, D), (FF // 2) ** -0.5, 0.25),
        "norm_final": jnp.clip(1.0 + 0.18 * jax.random.normal(splits[15], (D,), jnp.float32), 0.1, 1.9),
        "w_read": gaussian(splits[16], (D, 2), D ** -0.5, 0.375),
    }


def rms_scale(hidden, gain):
    mean_square = lax.optimization_barrier(jnp.mean(hidden * hidden, axis=-1, keepdims=True))
    return hidden * lax.rsqrt(mean_square + 1e-06) * gain

def embed(syndrome, events, boundary, syn_table, event_table, bound_table, pos_table):
    synd_bits = syndrome.astype(jnp.float32)[..., None]
    event_bits = events.astype(jnp.float32)[..., None]
    start = syn_table[0] + synd_bits * (syn_table[1] - syn_table[0])
    start = start + event_table[0] + event_bits * (event_table[1] - event_table[0])
    for kind in range(bound_table.shape[0]):
        chosen = (boundary == kind).astype(jnp.float32)[..., None]
        start = start + chosen * bound_table[kind]
    rows = start.reshape(start.shape[0], -1, pos_table.shape[0], start.shape[-1])
    return rows + pos_table

def attend_row(query_row, key_rows, value_rows, row_valid, dilation, heads):
    tiles, tile_len, width = query_row.shape
    head_dim = width // heads
    padding = ((0, 0), (dilation, dilation), (0, 0), (0, 0))
    key_pad = jnp.pad(key_rows, padding)
    value_pad = jnp.pad(value_rows, padding)

    def one_block(block_index):
        start = block_index * 8
        key_win = lax.dynamic_slice_in_dim(key_pad, start, 8 + 2 * dilation, 1)
        value_win = lax.dynamic_slice_in_dim(value_pad, start, 8 + 2 * dilation, 1)
        query_blk = lax.dynamic_slice_in_dim(query_row, start, 8, 0)
        key_list = []
        value_list = []
        for source in range(3):
            for column in range(3):
                key_list.append(key_win[source, column * dilation:column * dilation + 8])
                value_list.append(value_win[source, column * dilation:column * dilation + 8])
        key_all = jnp.stack(key_list, axis=1).reshape(8, 9 * tile_len, heads, head_dim)
        value_all = jnp.stack(value_list, axis=1).reshape(8, 9 * tile_len, heads, head_dim)
        query_heads = query_blk.reshape(8, tile_len, heads, head_dim)
        scores = jnp.einsum('tqhe,tkhe->thqk', query_heads.astype(jnp.float32), key_all.astype(jnp.float32))
        scores = scores * (1.0 / float(head_dim) ** 0.5)
        tile_cols = start + jnp.arange(8, dtype=jnp.int32)
        col_list = []
        for column in range(3):
            shifted = tile_cols + (column - 1) * dilation
            col_list.append((shifted >= 0) & (shifted < tiles))
        col_valid = jnp.stack(col_list, axis=1)
        valid = row_valid[None, :, None] & col_valid[:, None, :]
        valid = jnp.repeat(valid.reshape(8, 9), tile_len, axis=1)
        scores = jnp.where(valid[:, None, None, :], scores, -1e+30)
        top = lax.optimization_barrier(jnp.max(scores, axis=-1, keepdims=True))
        expd = jnp.exp(scores - top)
        weights = (expd / lax.optimization_barrier(jnp.sum(expd, axis=-1, keepdims=True))).astype(jnp.bfloat16)
        mixed = jnp.einsum('thqk,tkhe->tqhe', weights.astype(jnp.float32), value_all.astype(jnp.float32))
        return mixed.astype(jnp.bfloat16).reshape(8, tile_len, width)
    blocks = lax.map(one_block, jnp.arange(tiles // 8, dtype=jnp.int32))
    return blocks.reshape(tiles, tile_len, width)

def project(inputs, weight):
    flat = inputs.reshape(-1, inputs.shape[-1])
    out = jnp.dot(flat, weight, preferred_element_type=jnp.float32).astype(jnp.bfloat16)
    return out.reshape(inputs.shape[:-1] + (weight.shape[1],))

def reference(syndrome, events, boundary, syn_table, event_table, bound_table, pos_table, norm_attn, w_query, w_key, w_value, w_out, norm_mlp, w_up, w_down, norm_final, w_read):
    stream = embed(syndrome, events, boundary, syn_table, event_table, bound_table, pos_table)
    width = stream.shape[-1]
    row_count = stream.shape[0]
    for layer in range(LAYERS):
        dilation = layer + 1
        normed = rms_scale(stream, norm_attn[layer]).astype(jnp.bfloat16)
        queries = project(normed, w_query[layer])
        keys = project(normed, w_key[layer])
        values = project(normed, w_value[layer])
        padding = ((dilation, dilation), (0, 0), (0, 0), (0, 0))
        key_pad = jnp.pad(keys, padding)
        value_pad = jnp.pad(values, padding)

        def one_row(row_index):
            key_span = lax.dynamic_slice_in_dim(key_pad, row_index, 2 * dilation + 1, 0)
            value_span = lax.dynamic_slice_in_dim(value_pad, row_index, 2 * dilation + 1, 0)
            key_rows = jnp.stack([key_span[0], key_span[dilation], key_span[2 * dilation]])
            value_rows = jnp.stack([value_span[0], value_span[dilation], value_span[2 * dilation]])
            row_valid = jnp.stack([row_index - dilation >= 0, row_index >= 0, row_index + dilation < row_count])
            query_row = lax.dynamic_index_in_dim(queries, row_index, 0, keepdims=False)
            return attend_row(query_row, key_rows, value_rows, row_valid, dilation, HEADS)
        attended = lax.map(one_row, jnp.arange(row_count, dtype=jnp.int32))
        stream = stream + jnp.dot(attended.reshape(-1, width), w_out[layer], preferred_element_type=jnp.float32).reshape(stream.shape)
        normed = rms_scale(stream, norm_mlp[layer]).astype(jnp.bfloat16)
        inner = jax.nn.gelu(jnp.dot(normed.reshape(-1, width), w_up[layer], preferred_element_type=jnp.float32), approximate=True).astype(jnp.bfloat16)
        stream = stream + jnp.dot(inner, w_down[layer], preferred_element_type=jnp.float32).reshape(stream.shape)
    final = rms_scale(stream, norm_final).astype(jnp.bfloat16)
    readout = jnp.dot(final.reshape(-1, width), w_read, preferred_element_type=jnp.float32)
    return readout.reshape(row_count, -1, 2).transpose(2, 0, 1)
```

```python
import functools
import math

import jax
import jax.numpy as jnp
from jax import lax
from jax.experimental import pallas as pl
from jax.experimental.pallas import tpu as pltpu
from jax.sharding import PartitionSpec as P

HEADS = 8
TILE = 64
CHUNK = 256
NEG = -1e30


def shifted(value, axis, steps):
    count = lax.axis_size(axis)
    first, last = (max(0, -steps), min(count, count - steps))
    return lax.ppermute(value, axis, [(source, source + steps) for source in range(first, last)])


def dot(a, b):
    return jnp.dot(a, b, preferred_element_type=jnp.float32)


def wide(t):
    return jnp.concatenate([t, t], axis=1)


def rms(x, gain):
    mean_square = jnp.mean(x * x, axis=0, keepdims=True)
    return x * lax.rsqrt(mean_square + 1e-06) * gain


def gelu(x):
    inner = math.sqrt(2.0 / math.pi) * (x + 0.044715 * (x * x * x))
    return 0.5 * x * (1.0 + jnp.tanh(inner))


def row_biases(dilation):
    me = lax.axis_index("lx")
    count = lax.axis_size("lx")
    low = jnp.where(me - dilation >= 0, 0.0, NEG).astype(jnp.float32)
    high = jnp.where(me + dilation < count, 0.0, NEG).astype(jnp.float32)
    return low, high


def write_keys(normed, wk, wvt, k_ref, v_ref, source, krow, vlane):
    keys = lax.dot_general(
        normed, wk, (((0,), (0,)), ((), ())), preferred_element_type=jnp.float32
    )
    k_ref[source, pl.ds(krow, CHUNK), :] = keys.astype(jnp.bfloat16)
    v_ref[source, :, pl.ds(vlane, CHUNK)] = dot(wvt, normed).astype(jnp.bfloat16)


def attend(q_chunk, k_ref, v_ref, krow, vlane, low, high, left, right, head_dim):
    scale = math.log2(math.e) / math.sqrt(head_dim)
    half = 4 * head_dim
    rows = lax.broadcasted_iota(jnp.int32, (half, CHUNK), 0) // head_dim
    cols = lax.broadcasted_iota(jnp.int32, (half, CHUNK), 1) // TILE
    diag = rows == cols
    zero_rows = jnp.zeros((TILE, CHUNK), jnp.bfloat16)
    tiles = []
    for t in range(4):
        q = q_chunk[:, TILE * t : TILE * t + TILE]
        q4 = wide(wide(q))
        parts = []
        for g in range(HEADS // 4):
            feats = slice(half * g, half * g + half)
            qg = jnp.where(diag, q4[feats], jnp.zeros((), jnp.bfloat16))
            scores = []
            for r in range(3):
                k_win = k_ref[r, pl.ds(krow + TILE * t, 3 * TILE), feats]
                s = dot(k_win, qg)
                for a in range(3):
                    part = s[TILE * a : TILE * a + TILE]
                    bias = None if r == 1 else (low if r == 0 else high)
                    if t == 0 and a == 0:
                        bias = left if bias is None else jnp.minimum(bias, left)
                    if t == 3 and a == 2:
                        bias = right if bias is None else jnp.minimum(bias, right)
                    scores.append(part if bias is None else part + bias)
            top = functools.reduce(
                jnp.maximum, [jnp.max(s, axis=0, keepdims=True) for s in scores]
            )
            exps = [jnp.exp2((s - top) * scale) for s in scores]
            total = functools.reduce(jnp.add, [jnp.sum(e, axis=0, keepdims=True) for e in exps])
            inv = 1.0 / total
            acc = None
            for r in range(3):
                w = [(e * inv).astype(jnp.bfloat16) for e in exps[3 * r : 3 * r + 3]]
                w = [zero_rows] + w if t % 2 == 0 else w + [zero_rows]
                lane = vlane + TILE * (t if t % 2 == 0 else t + 1)
                v_win = v_ref[r, feats, pl.ds(pl.multiple_of(lane, 128), CHUNK)]
                term = dot(v_win, jnp.concatenate(w, axis=0))
                acc = term if acc is None else acc + term
            for h in range(4):
                parts.append(
                    acc[head_dim * h : head_dim * h + head_dim, TILE * h : TILE * h + TILE]
                )
        tiles.append(jnp.concatenate(parts, axis=0))
    return jnp.concatenate(tiles, axis=1).astype(jnp.bfloat16)


def feed_forward(stream, gain, wut, wdt):
    normed = rms(stream, gain).astype(jnp.bfloat16)
    inner = gelu(dot(wut[...], normed)).astype(jnp.bfloat16)
    return stream + dot(wdt[...], inner)


def fill_tables(cols_ref, tab):
    for k in range(tab.shape[0]):
        tab[k] = jnp.broadcast_to(cols_ref[:, k : k + 1], tab.shape[1:])


def clear_pads(k_ref, v_ref, sections, sites):
    ks, vs = sites + 2 * TILE, sites + 256
    for sec in range(sections):
        for r in range(3):
            z = jnp.zeros((TILE, k_ref.shape[2]), k_ref.dtype)
            k_ref[r, sec * ks : sec * ks + TILE, :] = z
            k_ref[r, sec * ks + TILE + sites : sec * ks + 2 * TILE + sites, :] = z
            z = jnp.zeros((v_ref.shape[1], 128), v_ref.dtype)
            v_ref[r, :, sec * vs : sec * vs + 128] = z
            v_ref[r, :, sec * vs + 128 + sites : sec * vs + 256 + sites] = z


N_ATTN0, N_ATTN1, N_MLP0, N_MLP1, N_FINAL = range(6, 11)


def first_layer(
    own_ref, low_ref, high_ref, base_ref, cols_ref, wq_ref, wk_ref, wv_ref, wo_ref, wu_ref, wd_ref,
    stream_ref, normed_ref,
    tab, wqt, wvt, wot, wut, wdt, k_buf, v_buf, q_buf, x_buf,
):
    sites = own_ref.shape[1]
    width = base_ref.shape[0]
    fill_tables(cols_ref, tab)
    wqt[...] = wq_ref[0].T
    wvt[...] = wv_ref[0].T
    wot[...] = wo_ref[0].T
    wut[...] = wu_ref[0].T
    wdt[...] = wd_ref[0].T
    clear_pads(k_buf, v_buf, 1, sites)
    low, high = row_biases(1)
    chunks = sites // CHUNK

    def embed(ref, lane):
        syn = ref[0:1, pl.ds(lane, 128)].astype(jnp.float32)
        ev = ref[1:2, pl.ds(lane, 128)].astype(jnp.float32)
        bnd = ref[2:3, pl.ds(lane, 128)]
        x = base_ref[...] + syn * tab[0] + ev * tab[1]
        b = jnp.broadcast_to(bnd, x.shape)
        return x + jnp.where(
            b < 2, jnp.where(b == 0, tab[2], tab[3]), jnp.where(b == 2, tab[4], tab[5])
        )

    def project(c, carry):
        lane = pl.multiple_of(c * CHUNK, CHUNK)
        for r, ref in enumerate((low_ref, own_ref, high_ref)):
            x = jnp.concatenate([embed(ref, lane), embed(ref, lane + 128)], axis=1)
            n = rms(x, wide(tab[N_ATTN0])).astype(jnp.bfloat16)
            write_keys(n, wk_ref[0], wvt[...], k_buf, v_buf, r, lane + TILE, lane + 128)
            if r == 1:
                x_buf[:, pl.ds(lane, CHUNK)] = x
                q_buf[:, pl.ds(lane, CHUNK)] = dot(wqt[...], n).astype(jnp.bfloat16)
        return carry

    lax.fori_loop(0, chunks, project, 0)

    def block(c, carry):
        lane = pl.multiple_of(c * CHUNK, CHUNK)
        left = jnp.where(c > 0, 0.0, NEG).astype(jnp.float32)
        right = jnp.where(c < chunks - 1, 0.0, NEG).astype(jnp.float32)
        att = attend(
            q_buf[:, pl.ds(lane, CHUNK)], k_buf, v_buf, lane, lane, low, high, left, right,
            width // HEADS,
        )
        x = x_buf[:, pl.ds(lane, CHUNK)] + dot(wot[...], att)
        x = feed_forward(x, wide(tab[N_MLP0]), wut, wdt)
        n = rms(x, wide(tab[N_ATTN1]))
        for part in range(2):
            out = pl.multiple_of(part * (sites // 2) + c * 128, 128)
            b0, b1 = TILE * part, TILE * part + 128
            pick = lambda y: jnp.concatenate([y[:, b0 : b0 + TILE], y[:, b1 : b1 + TILE]], axis=1)
            stream_ref[:, pl.ds(out, 128)] = pick(x)
            normed_ref[:, pl.ds(out, 128)] = pick(n).astype(jnp.bfloat16)
        return carry

    lax.fori_loop(0, chunks, block, 0)


def second_layer(
    stream_ref, low_ref, own_ref, high_ref, cols_ref,
    wq_ref, wk_ref, wv_ref, wo_ref, wu_ref, wd_ref, wr_ref,
    out_ref,
    tab, wqt, wvt, wot, wut, wdt, k_buf, v_buf, q_buf,
):
    width, sites = stream_ref.shape
    half = sites // 2
    fill_tables(cols_ref, tab)
    wqt[...] = wq_ref[0].T
    wvt[...] = wv_ref[0].T
    wot[...] = wo_ref[0].T
    wut[...] = wu_ref[0].T
    wdt[...] = wd_ref[0].T
    clear_pads(k_buf, v_buf, 2, half)
    low, high = row_biases(2)
    chunks = sites // CHUNK
    per = chunks // 2

    def project(c, carry):
        lane = pl.multiple_of(c * CHUNK, CHUNK)
        sec = c // per
        krow = pl.multiple_of(sec * 2 * TILE + lane + TILE, TILE)
        vlane = pl.multiple_of(sec * 256 + lane + 128, 128)
        for r, ref in enumerate((low_ref, own_ref, high_ref)):
            n = ref[:, pl.ds(lane, CHUNK)]
            write_keys(n, wk_ref[0], wvt[...], k_buf, v_buf, r, krow, vlane)
            if r == 1:
                q_buf[:, pl.ds(lane, CHUNK)] = dot(wqt[...], n).astype(jnp.bfloat16)
        return carry

    lax.fori_loop(0, chunks, project, 0)

    def block(c, carry):
        lane = pl.multiple_of(c * CHUNK, CHUNK)
        sec = c // per
        local = c - sec * per
        krow = pl.multiple_of(sec * 2 * TILE + lane, TILE)
        vlane = pl.multiple_of(sec * 256 + lane, 128)
        left = jnp.where(local > 0, 0.0, NEG).astype(jnp.float32)
        right = jnp.where(local < per - 1, 0.0, NEG).astype(jnp.float32)
        att = attend(
            q_buf[:, pl.ds(lane, CHUNK)], k_buf, v_buf, krow, vlane, low, high, left, right,
            width // HEADS,
        )
        x = stream_ref[:, pl.ds(lane, CHUNK)] + dot(wot[...], att)
        x = feed_forward(x, wide(tab[N_MLP1]), wut, wdt)
        n = rms(x, wide(tab[N_FINAL])).astype(jnp.bfloat16)
        out_ref[:, pl.ds(lane, CHUNK)] = dot(wr_ref[...], n)
        return carry

    lax.fori_loop(0, chunks, block, 0)


def scratch(width, ff, sites, sections, ncols):
    local = sites // sections
    bf = jnp.bfloat16
    return [
        pltpu.VMEM((ncols, width, 128), jnp.float32),
        pltpu.VMEM((width, width), bf),
        pltpu.VMEM((width, width), bf),
        pltpu.VMEM((width, width), bf),
        pltpu.VMEM((ff, width), bf),
        pltpu.VMEM((width, ff), bf),
        pltpu.VMEM((3, sections * (local + 2 * TILE), width), bf),
        pltpu.VMEM((3, width, sections * (local + 256)), bf),
        pltpu.VMEM((width, sites), bf),
    ]


def on_device(
    syndrome, events, boundary, syn_table, event_table, bound_table, pos_table, norm_attn,
    w_query, w_key, w_value, w_out, norm_mlp, w_up, w_down, norm_final, w_read,
):
    sites = syndrome.shape[1]
    width = pos_table.shape[1]
    ff = w_up.shape[2]
    own = jnp.concatenate([syndrome, events, boundary], axis=0)
    low = shifted(own, "lx", 1)
    high = shifted(own, "lx", -1)
    cols = jnp.concatenate(
        [
            (syn_table[1] - syn_table[0])[None],
            (event_table[1] - event_table[0])[None],
            bound_table,
            norm_attn,
            norm_mlp,
            norm_final[None],
        ],
        axis=0,
    )
    ncols = cols.shape[0]
    cols = cols.T
    base = (pos_table + syn_table[0] + event_table[0]).T
    base = jnp.concatenate([base, base], axis=1)
    params = pltpu.CompilerParams(vmem_limit_bytes=48 * 1024 * 1024)

    vmem = pl.BlockSpec(memory_space=pltpu.VMEM)

    def weight(w, layer):
        return w[layer : layer + 1]

    ws = [w_query, w_key, w_value, w_out, w_up, w_down]
    stream, normed = pl.pallas_call(
        first_layer,
        name="first_layer",
        out_shape=(
            jax.ShapeDtypeStruct((width, sites), jnp.float32),
            jax.ShapeDtypeStruct((width, sites), jnp.bfloat16),
        ),
        in_specs=[vmem] * 11,
        out_specs=(vmem, vmem),
        scratch_shapes=scratch(width, ff, sites, 1, ncols)
        + [pltpu.VMEM((width, sites), jnp.float32)],
        compiler_params=params,
    )(own, low, high, base, cols, *[weight(w, 0) for w in ws])
    normed_low = shifted(normed, "lx", 2)
    normed_high = shifted(normed, "lx", -2)
    read = jnp.pad(w_read.T, ((0, 16 - w_read.shape[1]), (0, 0)))
    out = pl.pallas_call(
        second_layer,
        name="second_layer",
        out_shape=jax.ShapeDtypeStruct((16, sites), jnp.float32),
        in_specs=[vmem] * 12,
        out_specs=vmem,
        scratch_shapes=scratch(width, ff, sites, 2, ncols),
        compiler_params=params,
    )(stream, normed_low, normed, normed_high, cols, *[weight(w, 1) for w in ws], read)
    logits = out[:2].reshape(2, 2, sites // (2 * TILE), TILE).transpose(0, 2, 1, 3)
    return logits.reshape(2, 1, sites)


def solution(mesh):
    rows = P(("groups", "lx"), None)
    return jax.shard_map(
        on_device,
        mesh=mesh,
        in_specs=(rows,) * 3 + (P(),) * 14,
        out_specs=P(None, ("groups", "lx"), None),
        check_vma=False,
    )
```

```python
import functools
import math

import jax
import jax.numpy as jnp
from jax import lax
from jax.experimental import pallas as pl
from jax.experimental.pallas import tpu as pltpu
from jax.sharding import PartitionSpec as P

HEADS = 8
TILE = 64
CHUNK = 256
PAIR = 128
GROUP = 4
GROUPS = HEADS // GROUP
ONES = 16
BF = jnp.bfloat16
N_ATTN0, N_ATTN1, N_MLP0, N_MLP1, N_FINAL = range(6, 11)


def dot(a, b):
    return jnp.dot(a, b, preferred_element_type=jnp.float32)


def wide(t):
    return jnp.concatenate([t, t], axis=1)


def rms(x, gain):
    mean_square = jnp.mean(x * x, axis=0, keepdims=True)
    return x * lax.rsqrt(mean_square + 1e-06) * gain


def gelu(x):
    inner = math.sqrt(2.0 / math.pi) * (x + 0.044715 * (x * x * x))
    return 0.5 * x * (1.0 + jnp.tanh(inner))


def attend(q_chunk, k_ref, v_ref, sec, base, head_dim):
    scale = math.log2(math.e) / math.sqrt(head_dim)
    half = GROUP * head_dim
    rows = lax.broadcasted_iota(jnp.int32, (half, CHUNK), 0) // head_dim
    cols = lax.broadcasted_iota(jnp.int32, (half, CHUNK), 1) // TILE
    diag = rows == cols
    zero_rows = jnp.zeros((TILE, CHUNK), BF)
    units = [(t, g) for t in range(4) for g in range(GROUPS)]
    tile_q = [wide(wide(q_chunk[:, TILE * t : TILE * t + TILE])) for t in range(4)]

    def scores(t, g):
        feats = slice(half * g, half * g + half)
        qg = jnp.where(diag, tile_q[t][feats], jnp.zeros((), BF))
        return [
            dot(k_ref[r, sec, pl.ds(base + TILE * t, 3 * TILE), feats], qg) for r in range(3)
        ]

    def mix(t, g, s):
        top = functools.reduce(jnp.maximum, [jnp.max(p, axis=0, keepdims=True) for p in s])
        acc = None
        for r in range(3):
            e = jnp.exp2((s[r] - top) * scale).astype(BF)
            e = jnp.concatenate([zero_rows, e] if t % 2 == 0 else [e, zero_rows], axis=0)
            lane = pl.multiple_of(base + TILE * (t if t % 2 == 0 else t + 1), 128)
            term = dot(v_ref[r, sec, g, :, pl.ds(lane, CHUNK)], e)
            acc = term if acc is None else acc + term
        acc = acc[:half] * (1.0 / acc[half : half + 1])
        return [
            acc[head_dim * h : head_dim * h + head_dim, TILE * h : TILE * h + TILE]
            for h in range(GROUP)
        ]

    parts = [[] for _ in range(4)]
    now = scores(*units[0])
    for i, (t, g) in enumerate(units):
        later = scores(*units[i + 1]) if i + 1 < len(units) else None
        parts[t] += mix(t, g, now)
        now = later
    return jnp.concatenate([jnp.concatenate(p, axis=0) for p in parts], axis=1).astype(BF)


def feed_forward(stream, gain, wut, wdt):
    normed = rms(stream, gain).astype(BF)
    inner = gelu(dot(wut, normed)).astype(BF)
    return stream + dot(wdt, inner)


def decoder(
    syn_ref, ev_ref, bnd_ref, synt_ref, evt_ref, bt_ref, pos_ref, na_ref,
    wq_ref, wk_ref, wv_ref, wo_ref, nm_ref, wu_ref, wd_ref, nf_ref, wr_ref,
    out_ref,
    tab, base, wqt, wvt, wot, wut, wdt, bits, nbuf, x0, q0, k0, v0, x1, q1, k1, v1, logit,
    bit_send, bit_recv, n_send, n_recv,
):
    me = lax.axis_index("lx")
    count = lax.axis_size("lx")
    sites = syn_ref.shape[1]
    width = pos_ref.shape[1]
    head_dim = width // HEADS
    half = GROUP * head_dim
    chunks = sites // CHUNK
    local = sites // 2
    per = chunks // 2
    exists = {
        (d, r): (me - d >= 0) if r == 0 else (me + d < count) for d in (1, 2) for r in (0, 2)
    }
    where_to = {(d, r): me - d if r == 0 else me + d for d in (1, 2) for r in (0, 2)}

    barrier = pltpu.get_barrier_semaphore()
    total = jnp.int32(0)
    for key, there in exists.items():
        total = total + there.astype(jnp.int32)

        @pl.when(there)
        def _():
            pl.semaphore_signal(
                barrier, inc=1, device_id={"lx": where_to[key]},
                device_id_type=pl.DeviceIdType.MESH,
            )

    bits[1] = jnp.concatenate(
        [syn_ref[...], ev_ref[...], bnd_ref[...], jnp.zeros((5, sites), jnp.int32)], axis=0
    )
    pl.semaphore_wait(barrier, total)

    def bit_copy(r):
        return pltpu.make_async_remote_copy(
            src_ref=bits.at[1], dst_ref=bits.at[2 - r],
            send_sem=bit_send.at[r // 2], recv_sem=bit_recv.at[(2 - r) // 2],
            device_id={"lx": where_to[1, r]}, device_id_type=pl.DeviceIdType.MESH,
        )

    def bit_arrival(r):
        return pltpu.make_async_remote_copy(
            src_ref=bits.at[1], dst_ref=bits.at[r],
            send_sem=bit_send.at[r // 2], recv_sem=bit_recv.at[r // 2],
            device_id={"lx": where_to[1, r]}, device_id_type=pl.DeviceIdType.MESH,
        )

    def row_copy(r, c):
        return pltpu.make_async_remote_copy(
            src_ref=nbuf.at[1, c], dst_ref=nbuf.at[2 - r, c],
            send_sem=n_send.at[r // 2, c], recv_sem=n_recv.at[(2 - r) // 2, c],
            device_id={"lx": where_to[2, r]}, device_id_type=pl.DeviceIdType.MESH,
        )

    def row_arrival(r, c):
        return pltpu.make_async_remote_copy(
            src_ref=nbuf.at[1, c], dst_ref=nbuf.at[r, c],
            send_sem=n_send.at[r // 2, c], recv_sem=n_recv.at[r // 2, c],
            device_id={"lx": where_to[2, r]}, device_id_type=pl.DeviceIdType.MESH,
        )

    for r in (0, 2):

        @pl.when(exists[1, r])
        def _():
            bit_copy(r).start()

        @pl.when(jnp.logical_not(exists[1, r]))
        def _():
            bits[r] = bits[1]

    cols = jnp.concatenate(
        [
            synt_ref[1:2] - synt_ref[0:1], evt_ref[1:2] - evt_ref[0:1], bt_ref[...],
            na_ref[...], nm_ref[...], nf_ref[...], jnp.zeros((5, width), jnp.float32),
        ],
        axis=0,
    ).T
    for k in range(tab.shape[0]):
        tab[k] = jnp.broadcast_to(cols[:, k : k + 1], tab.shape[1:])
    start = pos_ref[...] + synt_ref[0:1] + evt_ref[0:1]
    base[...] = jnp.concatenate([start, start], axis=0).T
    for layer in range(2):
        wqt[layer] = wq_ref[layer].T
        wvt[layer] = wv_ref[layer].T
        wot[layer] = wo_ref[layer].T
        wut[layer] = wu_ref[layer].T
        wdt[layer] = wd_ref[layer].T

    def valid(d, r):
        return jnp.float32(1.0) if r == 1 else jnp.where(exists[d, r], 1.0, 0.0).astype(jnp.float32)

    for d, v_ref in ((1, v0), (2, v1)):
        length = v_ref.shape[4]
        for r in range(3):
            flag = jnp.full((ONES, length - 2 * PAIR), 1.0, jnp.float32) * valid(d, r)
            for sec in range(v_ref.shape[1]):
                for g in range(GROUPS):
                    zero = jnp.zeros((half + ONES, PAIR), BF)
                    v_ref[r, sec, g, :, 0:PAIR] = zero
                    v_ref[r, sec, g, :, length - PAIR : length] = zero
                    v_ref[r, sec, g, half : half + ONES, PAIR : length - PAIR] = flag.astype(BF)

    def keys_of(n, layer):
        keys = lax.dot_general(
            n, wk_ref[layer], (((0,), (0,)), ((), ())), preferred_element_type=jnp.float32
        )
        return keys.astype(BF)

    def embed(r, lane):
        syn = bits[r, 0:1, pl.ds(lane, PAIR)].astype(jnp.float32)
        ev = bits[r, 1:2, pl.ds(lane, PAIR)].astype(jnp.float32)
        x = base[...] + syn * tab[0] + ev * tab[1]
        b = jnp.broadcast_to(bits[r, 2:3, pl.ds(lane, PAIR)], x.shape)
        return x + jnp.where(
            b < 2, jnp.where(b == 0, tab[2], tab[3]), jnp.where(b == 2, tab[4], tab[5])
        )

    def project0(sources, c, carry):
        lane = pl.multiple_of(c * CHUNK, CHUNK)
        for r in sources:
            x = jnp.concatenate([embed(r, lane), embed(r, lane + PAIR)], axis=1)
            n = rms(x, wide(tab[N_ATTN0])).astype(BF)
            k0[r, 0, pl.ds(lane + TILE, CHUNK), :] = keys_of(n, 0)
            v = dot(wvt[0], n)
            if r == 1:
                x0[:, pl.ds(lane, CHUNK)] = x
                q0[:, pl.ds(lane, CHUNK)] = dot(wqt[0], n).astype(BF)
            else:
                v = v * valid(1, r)
            for g in range(GROUPS):
                v0[r, 0, g, 0:half, pl.ds(lane + PAIR, CHUNK)] = v[
                    half * g : half * g + half
                ].astype(BF)
        return carry

    lax.fori_loop(0, chunks, functools.partial(project0, (1,)), 0)
    for r in (0, 2):

        @pl.when(exists[1, r])
        def _():
            bit_arrival(r).wait_recv()

    lax.fori_loop(0, chunks, functools.partial(project0, (0, 2)), 0)
    for r in range(3):
        k0[r, 0, 0:TILE, :] = k0[r, 0, TILE : 2 * TILE, :]
        k0[r, 0, sites + TILE : sites + 2 * TILE, :] = k0[r, 0, sites : sites + TILE, :]

    def project1(r, c, n):
        lane = pl.multiple_of(c * PAIR, PAIR)
        keys = keys_of(n, 1)
        v = dot(wvt[1], n)
        if r == 1:
            q = dot(wqt[1], n).astype(BF)
        else:
            v = v * valid(2, r)
        v = v.astype(BF)
        for sec in range(2):
            part = slice(PAIR * sec, PAIR * sec + PAIR)
            k1[r, sec, pl.ds(lane + TILE, PAIR), :] = keys[part]
            for g in range(GROUPS):
                v1[r, sec, g, 0:half, pl.ds(lane + PAIR, PAIR)] = v[half * g : half * g + half, part]
            if r == 1:
                q1[sec, :, pl.ds(lane, PAIR)] = q[:, part]

    def block0(c, carry):
        lane = pl.multiple_of(c * CHUNK, CHUNK)
        att = attend(q0[:, pl.ds(lane, CHUNK)], k0, v0, 0, lane, head_dim)
        x = x0[:, pl.ds(lane, CHUNK)] + dot(wot[0], att)
        x = feed_forward(x, wide(tab[N_MLP0]), wut[0], wdt[0])
        x = jnp.concatenate(
            [x[:, TILE * t : TILE * t + TILE] for t in (0, 2, 1, 3)], axis=1
        )
        n = rms(x, wide(tab[N_ATTN1])).astype(BF)
        out = pl.multiple_of(c * PAIR, PAIR)
        for sec in range(2):
            part = slice(PAIR * sec, PAIR * sec + PAIR)
            x1[sec, :, pl.ds(out, PAIR)] = x[:, part]
            nbuf[1, c, sec] = n[:, part]
        for r in (0, 2):

            @pl.when(exists[2, r])
            def _():
                row_copy(r, c).start()

            @pl.when(jnp.logical_not(exists[2, r]))
            def _():
                for sec in range(2):
                    nbuf[r, c, sec] = n[:, PAIR * sec : PAIR * sec + PAIR]

        project1(1, c, n)
        return carry

    lax.fori_loop(0, chunks, block0, 0)

    def arrive(c, carry):
        for r in (0, 2):

            @pl.when(exists[2, r])
            def _():
                row_arrival(r, c).wait_recv()

            project1(r, c, jnp.concatenate([nbuf[r, c, 0], nbuf[r, c, 1]], axis=1))
        return carry

    arrive(0, 0)
    for r in range(3):
        for sec in range(2):
            k1[r, sec, 0:TILE, :] = k1[r, sec, TILE : 2 * TILE, :]

    def block1(cc, carry):
        lax.fori_loop(2 * cc + 1, jnp.minimum(2 * cc + 3, chunks), arrive, 0)

        @pl.when(cc == per - 1)
        def _():
            for r in range(3):
                for sec in range(2):
                    k1[r, sec, local + TILE : local + 2 * TILE, :] = k1[
                        r, sec, local : local + TILE, :
                    ]

        lane = pl.multiple_of(cc * CHUNK, CHUNK)

        def section(sec, inner_carry):
            att = attend(q1[sec, :, pl.ds(lane, CHUNK)], k1, v1, sec, lane, head_dim)
            x = x1[sec, :, pl.ds(lane, CHUNK)] + dot(wot[1], att)
            x = feed_forward(x, wide(tab[N_MLP1]), wut[1], wdt[1])
            n = rms(x, wide(tab[N_FINAL])).astype(BF)
            logit[sec] = dot(wr_ref[...], n)
            return inner_carry

        lax.fori_loop(0, 2, section, 0)
        woven = []
        for t in range(CHUNK // TILE):
            woven += [logit[sec, :, TILE * t : TILE * t + TILE] for sec in range(2)]
        out_ref[:, pl.ds(pl.multiple_of(cc * 2 * CHUNK, 2 * CHUNK), 2 * CHUNK)] = jnp.concatenate(
            woven, axis=1
        )
        return carry

    lax.fori_loop(0, per, block1, 0)

    for r in (0, 2):

        @pl.when(exists[1, r])
        def _():
            bit_copy(r).wait_send()

        @pl.when(exists[2, r])
        def _():
            def sent(c, carry):
                row_copy(r, c).wait_send()
                return carry

            lax.fori_loop(0, chunks, sent, 0)


def on_device(
    syndrome, events, boundary, syn_table, event_table, bound_table, pos_table, norm_attn,
    w_query, w_key, w_value, w_out, norm_mlp, w_up, w_down, norm_final, w_read,
):
    sites = syndrome.shape[1]
    width = pos_table.shape[1]
    ff = w_up.shape[2]
    chunks = sites // CHUNK
    half = width // GROUPS
    vmem = pl.BlockSpec(memory_space=pltpu.VMEM)
    f32 = jnp.float32

    def attention_buffers(sections):
        local = sites // sections
        return [
            pltpu.VMEM((3, sections, local + 2 * TILE, width), BF),
            pltpu.VMEM((3, sections, GROUPS, half + ONES, local + 2 * PAIR), BF),
        ]

    outs = w_read.shape[1]
    logits = pl.pallas_call(
        decoder,
        name="decoder",
        out_shape=jax.ShapeDtypeStruct((outs, sites), f32),
        in_specs=[vmem] * 17,
        out_specs=vmem,
        scratch_shapes=[
            pltpu.VMEM((11, width, PAIR), f32),
            pltpu.VMEM((width, PAIR), f32),
            pltpu.VMEM((2, width, width), BF),
            pltpu.VMEM((2, width, width), BF),
            pltpu.VMEM((2, width, width), BF),
            pltpu.VMEM((2, ff, width), BF),
            pltpu.VMEM((2, width, ff), BF),
            pltpu.VMEM((3, 8, sites), jnp.int32),
            pltpu.VMEM((3, chunks, 2, width, PAIR), BF),
            pltpu.VMEM((width, sites), f32),
            pltpu.VMEM((width, sites), BF),
            *attention_buffers(1),
            pltpu.VMEM((2, width, sites // 2), f32),
            pltpu.VMEM((2, width, sites // 2), BF),
            *attention_buffers(2),
            pltpu.VMEM((2, outs, CHUNK), f32),
            pltpu.SemaphoreType.DMA((2,)),
            pltpu.SemaphoreType.DMA((2,)),
            pltpu.SemaphoreType.DMA((2, chunks)),
            pltpu.SemaphoreType.DMA((2, chunks)),
        ],
        compiler_params=pltpu.CompilerParams(
            vmem_limit_bytes=56 * 1024 * 1024, collective_id=0, has_side_effects=True
        ),
    )(
        syndrome, events, boundary, syn_table, event_table, bound_table, pos_table, norm_attn,
        w_query, w_key, w_value, w_out, norm_mlp, w_up, w_down, norm_final[None], w_read.T,
    )
    return logits[:, None, :]


def solution(mesh):
    rows = P(("groups", "lx"), None)
    return jax.shard_map(
        on_device,
        mesh=mesh,
        in_specs=(rows,) * 3 + (P(),) * 14,
        out_specs=P(None, ("groups", "lx"), None),
        check_vma=False,
    )
```

```python
import functools
import math

import jax
import jax.numpy as jnp
from jax import lax
from jax.experimental import pallas as pl
from jax.experimental.pallas import tpu as pltpu
from jax.sharding import PartitionSpec as P

HEADS = 8
TILE = 64
CHUNK = 256
PAIR = 128
GROUP = 4
GROUPS = HEADS // GROUP
ONES = 16
BF = jnp.bfloat16
N_ATTN0, N_ATTN1, N_MLP0, N_MLP1, N_FINAL = range(6, 11)


def dot(a, b):
    return jnp.dot(a, b, preferred_element_type=jnp.float32)


def wide(t):
    return jnp.concatenate([t, t], axis=1)


def rms(x, gain):
    mean_square = jnp.mean(x * x, axis=0, keepdims=True)
    return x * lax.rsqrt(mean_square + 1e-06) * gain


def gelu(x):
    inner = math.sqrt(2.0 / math.pi) * (x + 0.044715 * (x * x * x))
    return 0.5 * x * (1.0 + jnp.tanh(inner))


def attend(tiles, k_ref, v_ref, head_dim):
    scale = math.log2(math.e) / math.sqrt(head_dim)
    half = GROUP * head_dim
    rows = lax.broadcasted_iota(jnp.int32, (half, CHUNK), 0) // head_dim
    cols = lax.broadcasted_iota(jnp.int32, (half, CHUNK), 1) // TILE
    diag = rows == cols
    zero_rows = jnp.zeros((TILE, CHUNK), BF)

    def scores(q, sec, base, t):
        q4 = wide(wide(q))
        out = []
        for g in range(GROUPS):
            feats = slice(half * g, half * g + half)
            qg = jnp.where(diag, q4[feats], jnp.zeros((), BF))
            out.append(
                [dot(k_ref[r, sec, pl.ds(base + TILE * t, 3 * TILE), feats], qg) for r in range(3)]
            )
        return out

    def soften(s):
        top = functools.reduce(jnp.maximum, [jnp.max(p, axis=0, keepdims=True) for p in s])
        return [jnp.exp2((p - top) * scale).astype(BF) for p in s]

    def mix(exps, sec, base, t):
        parts = []
        for g in range(GROUPS):
            acc = None
            for r in range(3):
                e = exps[g][r]
                e = jnp.concatenate([zero_rows, e] if t % 2 == 0 else [e, zero_rows], axis=0)
                lane = pl.multiple_of(base + TILE * (t if t % 2 == 0 else t + 1), 128)
                term = dot(v_ref[r, sec, g, :, pl.ds(lane, CHUNK)], e)
                acc = term if acc is None else acc + term
            acc = acc[:half] * (1.0 / acc[half : half + 1])
            parts += [
                acc[head_dim * h : head_dim * h + head_dim, TILE * h : TILE * h + TILE]
                for h in range(GROUP)
            ]
        return jnp.concatenate(parts, axis=0)

    outs = []
    now, before = scores(*tiles[0]), None
    for i in range(len(tiles)):
        later = scores(*tiles[i + 1]) if i + 1 < len(tiles) else None
        exps = [soften(s) for s in now]
        if before is not None:
            outs.append(mix(before, *tiles[i - 1][1:]))
        now, before = later, exps
    outs.append(mix(before, *tiles[-1][1:]))
    return jnp.concatenate(outs, axis=1).astype(BF)


def feed_forward(stream, gain, wut, wdt):
    normed = rms(stream, gain).astype(BF)
    inner = gelu(dot(wut, normed)).astype(BF)
    return stream + dot(wdt, inner)


def decoder(
    syn_ref, ev_ref, bnd_ref, synt_ref, evt_ref, bt_ref, pos_ref, na_ref,
    wq_ref, wk_ref, wv_ref, wo_ref, nm_ref, wu_ref, wd_ref, nf_ref, wr_ref,
    out_ref,
    tab, base, wqt, wvt, wot, wut, wdt, bits, nbuf, x0, q0, k0, v0, x1, q1, k1, v1,
    bit_send, bit_recv, n_send, n_recv,
):
    me = lax.axis_index("lx")
    count = lax.axis_size("lx")
    sites = syn_ref.shape[1]
    width = pos_ref.shape[1]
    head_dim = width // HEADS
    half = GROUP * head_dim
    chunks = sites // CHUNK
    local = sites // 2
    per = chunks // 2
    exists = {
        (d, r): (me - d >= 0) if r == 0 else (me + d < count) for d in (1, 2) for r in (0, 2)
    }
    where_to = {(d, r): me - d if r == 0 else me + d for d in (1, 2) for r in (0, 2)}

    barrier = pltpu.get_barrier_semaphore()
    total = jnp.int32(0)
    for key, there in exists.items():
        total = total + there.astype(jnp.int32)

        @pl.when(there)
        def _():
            pl.semaphore_signal(
                barrier, inc=1, device_id={"lx": where_to[key]},
                device_id_type=pl.DeviceIdType.MESH,
            )

    bits[1] = jnp.concatenate(
        [syn_ref[...], ev_ref[...], bnd_ref[...], jnp.zeros((5, sites), jnp.int32)], axis=0
    )
    pl.semaphore_wait(barrier, total)

    def bit_copy(r):
        return pltpu.make_async_remote_copy(
            src_ref=bits.at[1], dst_ref=bits.at[2 - r],
            send_sem=bit_send.at[r // 2], recv_sem=bit_recv.at[(2 - r) // 2],
            device_id={"lx": where_to[1, r]}, device_id_type=pl.DeviceIdType.MESH,
        )

    def bit_arrival(r):
        return pltpu.make_async_remote_copy(
            src_ref=bits.at[1], dst_ref=bits.at[r],
            send_sem=bit_send.at[r // 2], recv_sem=bit_recv.at[r // 2],
            device_id={"lx": where_to[1, r]}, device_id_type=pl.DeviceIdType.MESH,
        )

    def row_copy(r, c):
        return pltpu.make_async_remote_copy(
            src_ref=nbuf.at[1, c], dst_ref=nbuf.at[2 - r, c],
            send_sem=n_send.at[r // 2, c], recv_sem=n_recv.at[(2 - r) // 2, c],
            device_id={"lx": where_to[2, r]}, device_id_type=pl.DeviceIdType.MESH,
        )

    def row_arrival(r, c):
        return pltpu.make_async_remote_copy(
            src_ref=nbuf.at[1, c], dst_ref=nbuf.at[r, c],
            send_sem=n_send.at[r // 2, c], recv_sem=n_recv.at[r // 2, c],
            device_id={"lx": where_to[2, r]}, device_id_type=pl.DeviceIdType.MESH,
        )

    for r in (0, 2):

        @pl.when(exists[1, r])
        def _():
            bit_copy(r).start()

        @pl.when(jnp.logical_not(exists[1, r]))
        def _():
            bits[r] = bits[1]

    cols = jnp.concatenate(
        [
            synt_ref[1:2] - synt_ref[0:1], evt_ref[1:2] - evt_ref[0:1], bt_ref[...],
            na_ref[...], nm_ref[...], nf_ref[...], jnp.zeros((5, width), jnp.float32),
        ],
        axis=0,
    ).T
    for k in range(tab.shape[0]):
        tab[k] = jnp.broadcast_to(cols[:, k : k + 1], tab.shape[1:])
    start = pos_ref[...] + synt_ref[0:1] + evt_ref[0:1]
    base[...] = jnp.concatenate([start, start], axis=0).T
    for layer in range(2):
        wqt[layer] = wq_ref[layer].T
        wvt[layer] = wv_ref[layer].T
        wot[layer] = wo_ref[layer].T
        wut[layer] = wu_ref[layer].T
        wdt[layer] = wd_ref[layer].T

    def valid(d, r):
        return jnp.float32(1.0) if r == 1 else jnp.where(exists[d, r], 1.0, 0.0).astype(jnp.float32)

    for d, v_ref in ((1, v0), (2, v1)):
        length = v_ref.shape[4]
        for r in range(3):
            flag = jnp.full((ONES, length - 2 * PAIR), 1.0, jnp.float32) * valid(d, r)
            for sec in range(v_ref.shape[1]):
                for g in range(GROUPS):
                    zero = jnp.zeros((half + ONES, PAIR), BF)
                    v_ref[r, sec, g, :, 0:PAIR] = zero
                    v_ref[r, sec, g, :, length - PAIR : length] = zero
                    v_ref[r, sec, g, half : half + ONES, PAIR : length - PAIR] = flag.astype(BF)

    def keys_of(n, layer):
        keys = lax.dot_general(
            n, wk_ref[layer], (((0,), (0,)), ((), ())), preferred_element_type=jnp.float32
        )
        return keys.astype(BF)

    def embed(r, lane):
        syn = bits[r, 0:1, pl.ds(lane, PAIR)].astype(jnp.float32)
        ev = bits[r, 1:2, pl.ds(lane, PAIR)].astype(jnp.float32)
        x = base[...] + syn * tab[0] + ev * tab[1]
        b = jnp.broadcast_to(bits[r, 2:3, pl.ds(lane, PAIR)], x.shape)
        return x + jnp.where(
            b < 2, jnp.where(b == 0, tab[2], tab[3]), jnp.where(b == 2, tab[4], tab[5])
        )

    def project0(sources, c, carry):
        lane = pl.multiple_of(c * CHUNK, CHUNK)
        for r in sources:
            x = jnp.concatenate([embed(r, lane), embed(r, lane + PAIR)], axis=1)
            n = rms(x, wide(tab[N_ATTN0])).astype(BF)
            k0[r, 0, pl.ds(lane + TILE, CHUNK), :] = keys_of(n, 0)
            v = dot(wvt[0], n)
            if r == 1:
                x0[:, pl.ds(lane, CHUNK)] = x
                q0[:, pl.ds(lane, CHUNK)] = dot(wqt[0], n).astype(BF)
            else:
                v = v * valid(1, r)
            for g in range(GROUPS):
                v0[r, 0, g, 0:half, pl.ds(lane + PAIR, CHUNK)] = v[
                    half * g : half * g + half
                ].astype(BF)
        return carry

    lax.fori_loop(0, chunks, functools.partial(project0, (1,)), 0)
    for r in (0, 2):

        @pl.when(exists[1, r])
        def _():
            bit_arrival(r).wait_recv()

    lax.fori_loop(0, chunks, functools.partial(project0, (0, 2)), 0)
    for r in range(3):
        k0[r, 0, 0:TILE, :] = k0[r, 0, TILE : 2 * TILE, :]
        k0[r, 0, sites + TILE : sites + 2 * TILE, :] = k0[r, 0, sites : sites + TILE, :]

    def project1(r, c, n):
        lane = pl.multiple_of(c * CHUNK, CHUNK)
        keys = keys_of(n, 1)
        v = dot(wvt[1], n)
        if r == 1:
            q = dot(wqt[1], n).astype(BF)
        else:
            v = v * valid(2, r)
        v = v.astype(BF)
        for sec in range(2):
            part = slice(CHUNK * sec, CHUNK * sec + CHUNK)
            k1[r, sec, pl.ds(lane + TILE, CHUNK), :] = keys[part]
            for g in range(GROUPS):
                v1[r, sec, g, 0:half, pl.ds(lane + PAIR, CHUNK)] = v[half * g : half * g + half, part]
            if r == 1:
                q1[sec, :, pl.ds(lane, CHUNK)] = q[:, part]

    def cut(q):
        return [q[:, TILE * t : TILE * t + TILE] for t in range(q.shape[1] // TILE)]

    def block0(c, carry):
        lane = pl.multiple_of(c * 2 * CHUNK, 2 * CHUNK)
        q = cut(q0[:, pl.ds(lane, 2 * CHUNK)])
        att = attend([(q[t], 0, lane, t) for t in range(len(q))], k0, v0, head_dim)
        x = x0[:, pl.ds(lane, 2 * CHUNK)] + dot(wot[0], att)
        x = feed_forward(x, tab4(N_MLP0), wut[0], wdt[0])
        x = cut(x)
        x = jnp.concatenate(x[0::2] + x[1::2], axis=1)
        n = rms(x, tab4(N_ATTN1)).astype(BF)
        out = pl.multiple_of(c * CHUNK, CHUNK)
        for sec in range(2):
            part = slice(CHUNK * sec, CHUNK * sec + CHUNK)
            x1[sec, :, pl.ds(out, CHUNK)] = x[:, part]
            nbuf[1, c, sec] = n[:, part]
        for r in (0, 2):

            @pl.when(exists[2, r])
            def _():
                row_copy(r, c).start()

            @pl.when(jnp.logical_not(exists[2, r]))
            def _():
                for sec in range(2):
                    nbuf[r, c, sec] = n[:, CHUNK * sec : CHUNK * sec + CHUNK]

        project1(1, c, n)
        return carry

    def tab4(k):
        return wide(wide(tab[k]))

    lax.fori_loop(0, per, block0, 0)

    def arrive(c, carry):
        for r in (0, 2):

            @pl.when(exists[2, r])
            def _():
                row_arrival(r, c).wait_recv()

            project1(r, c, jnp.concatenate([nbuf[r, c, 0], nbuf[r, c, 1]], axis=1))
        return carry

    arrive(0, 0)
    for r in range(3):
        for sec in range(2):
            k1[r, sec, 0:TILE, :] = k1[r, sec, TILE : 2 * TILE, :]

    def block1(cc, carry):
        lax.fori_loop(cc + 1, jnp.minimum(cc + 2, per), arrive, 0)

        @pl.when(cc == per - 1)
        def _():
            for r in range(3):
                for sec in range(2):
                    k1[r, sec, local + TILE : local + 2 * TILE, :] = k1[
                        r, sec, local : local + TILE, :
                    ]

        lane = pl.multiple_of(cc * CHUNK, CHUNK)
        tiles = []
        for sec in range(2):
            q = cut(q1[sec, :, pl.ds(lane, CHUNK)])
            tiles += [(q[t], sec, lane, t) for t in range(len(q))]
        att = attend(tiles, k1, v1, head_dim)
        x = jnp.concatenate([x1[sec, :, pl.ds(lane, CHUNK)] for sec in range(2)], axis=1)
        x = feed_forward(x + dot(wot[1], att), tab4(N_MLP1), wut[1], wdt[1])
        n = rms(x, tab4(N_FINAL)).astype(BF)
        logit = cut(dot(wr_ref[...], n))
        count_of = len(logit) // 2
        woven = []
        for t in range(count_of):
            woven += [logit[t], logit[count_of + t]]
        out_ref[:, pl.ds(pl.multiple_of(cc * 2 * CHUNK, 2 * CHUNK), 2 * CHUNK)] = jnp.concatenate(
            woven, axis=1
        )
        return carry

    lax.fori_loop(0, per, block1, 0)

    for r in (0, 2):

        @pl.when(exists[1, r])
        def _():
            bit_copy(r).wait_send()

        @pl.when(exists[2, r])
        def _():
            def sent(c, carry):
                row_copy(r, c).wait_send()
                return carry

            lax.fori_loop(0, per, sent, 0)


def on_device(
    syndrome, events, boundary, syn_table, event_table, bound_table, pos_table, norm_attn,
    w_query, w_key, w_value, w_out, norm_mlp, w_up, w_down, norm_final, w_read,
):
    sites = syndrome.shape[1]
    width = pos_table.shape[1]
    ff = w_up.shape[2]
    chunks = sites // CHUNK
    half = width // GROUPS
    vmem = pl.BlockSpec(memory_space=pltpu.VMEM)
    f32 = jnp.float32

    def attention_buffers(sections):
        local = sites // sections
        return [
            pltpu.VMEM((3, sections, local + 2 * TILE, width), BF),
            pltpu.VMEM((3, sections, GROUPS, half + ONES, local + 2 * PAIR), BF),
        ]

    outs = w_read.shape[1]
    logits = pl.pallas_call(
        decoder,
        name="decoder",
        out_shape=jax.ShapeDtypeStruct((outs, sites), f32),
        in_specs=[vmem] * 17,
        out_specs=vmem,
        scratch_shapes=[
            pltpu.VMEM((11, width, PAIR), f32),
            pltpu.VMEM((width, PAIR), f32),
            pltpu.VMEM((2, width, width), BF),
            pltpu.VMEM((2, width, width), BF),
            pltpu.VMEM((2, width, width), BF),
            pltpu.VMEM((2, ff, width), BF),
            pltpu.VMEM((2, width, ff), BF),
            pltpu.VMEM((3, 8, sites), jnp.int32),
            pltpu.VMEM((3, chunks // 2, 2, width, CHUNK), BF),
            pltpu.VMEM((width, sites), f32),
            pltpu.VMEM((width, sites), BF),
            *attention_buffers(1),
            pltpu.VMEM((2, width, sites // 2), f32),
            pltpu.VMEM((2, width, sites // 2), BF),
            *attention_buffers(2),
            pltpu.SemaphoreType.DMA((2,)),
            pltpu.SemaphoreType.DMA((2,)),
            pltpu.SemaphoreType.DMA((2, chunks // 2)),
            pltpu.SemaphoreType.DMA((2, chunks // 2)),
        ],
        compiler_params=pltpu.CompilerParams(
            vmem_limit_bytes=56 * 1024 * 1024, collective_id=0, has_side_effects=True
        ),
    )(
        syndrome, events, boundary, syn_table, event_table, bound_table, pos_table, norm_attn,
        w_query, w_key, w_value, w_out, norm_mlp, w_up, w_down, norm_final[None], w_read.T,
    )
    return logits[:, None, :]


def solution(mesh):
    rows = P(("groups", "lx"), None)
    return jax.shard_map(
        on_device,
        mesh=mesh,
        in_specs=(rows,) * 3 + (P(),) * 14,
        out_specs=P(None, ("groups", "lx"), None),
        check_vma=False,
    )
```
